256 devices in a mesh: tile: 64 (over y, z_hi, x), mode: 4 (over z_lo, core).
Axes of the slice: x: 4, y: 4, z: 8 (z_hi: 4, z_lo: 2; z = z_hi * 2 + z_lo), core: 2. Of those that a mesh axis runs over, the one named last changes fastest.
Arguments:
- object_tiles: float32 [64, 2, 2, 128, 128], P('tile'), may hold values from -1.5 to 1.5
- probe: float32 [16, 2, 128, 128], P('mode'), may hold values from -1 to 1
- propagator_phase: float32 [128, 128], replicated, may hold values from -3.140625 to 3.140625
- measured: float32 [256, 128, 128], P('tile'), may hold values from 0.25 to 2
- positions: int32 [256, 2], P('tile'), may hold values from 0 to 128, as said below
Outputs:
- updated_object: float32 [64, 2, 2, 128, 128], P('tile')
- intensity: float32 [256, 128, 128], P('tile')
The draws below stay inside these ranges and needn't reach their ends.
Inputs may be any that keep to these rules, and one draw needn't show every extreme that they name: `positions`: row and column of the top-left cell of a pattern's 128 x 128 window within its tile's extended region.
All inputs are finite; a program needn't handle non-finite values.
Results may differ from the reference program's by a relative error of at most 0.0003.
Values sent between devices are 32-bit elements; how exact they have to be, the bound alone decides.
A program may use at most 64 MiB of HBM per device.

```python
import math
import jax
import jax.numpy as jnp
from jax import lax

K = 128
CORE = 128
HALO = 64
SLICES = 2
SCANS = 2
STEPS = 2
TILE_COLS = 8
MODES = 16
TILES = 64
PATTERNS = 256


def draw_positions(key, part):
    span_size = CORE + 2 * HALO - K + 1
    key_rows = jax.random.fold_in(key, 11)
    key_cols = jax.random.fold_in(key, 23)
    key_edge = jax.random.fold_in(key, 37)
    rows_drawn = jax.random.randint(key_rows, (PATTERNS,), 0, span_size)
    cols_drawn = jax.random.randint(key_cols, (PATTERNS,), 0, span_size)
    near_edge = jax.random.randint(key_edge, (PATTERNS,), 0, HALO // 2)
    pattern_index = jnp.arange(PATTERNS, dtype=jnp.int32)
    scan_index = pattern_index % SCANS
    cols_drawn = jnp.where(scan_index == 0, near_edge, cols_drawn)
    cols_drawn = jnp.where(scan_index == 1, span_size - 1 - near_edge, cols_drawn)
    return jnp.stack([rows_drawn, cols_drawn], axis=1).astype(jnp.int32)


def levels(rng, dims, split, smallest, largest):
    def one(dim, parts):
        heights = jax.random.uniform(jax.random.fold_in(jax.random.fold_in(rng, 6), dim), (parts,), jnp.float32, smallest / len(split), largest / len(split))
        return jnp.repeat(jnp.exp(heights), dims[dim] // parts).reshape((-1,) + (1,) * (len(dims) - dim - 1))

    factor_of = one(*split[0])
    for cut in split[1:]:
        factor_of = factor_of * one(*cut)
    return factor_of


def scatter_about(rng, shape, spread, most, shards=(), held_as=jnp.bfloat16):
    entries = spread * jax.random.normal(rng, shape, jnp.float32)
    if shards:
        entries = entries * levels(rng, shape, shards, -0.22, 0.18)
    return jnp.clip(entries, -most, most).astype(held_as)


def setup_inputs(seed: int = 0) -> dict:
    streams_of = jax.random.split(jax.random.key(seed), 6)
    object_tiles = scatter_about(streams_of[0], (TILES, SLICES, 2, CORE, CORE), 0.3, 1.5, ((0, 64),), jnp.float32)
    probe = scatter_about(streams_of[1], (MODES, 2, K, K), 0.18, 1.0, ((0, 4),), jnp.float32)
    propagator_phase = jnp.clip(jax.random.uniform(streams_of[2], (K, K), jnp.float32, -3.140625, 3.140625), -3.140625, 3.140625)
    measured = jnp.clip(0.25 + 1.75 * jax.random.uniform(streams_of[3], (PATTERNS, K, K), jnp.float32) ** levels(streams_of[3], (PATTERNS, K, K), ((0, 64),), -0.2, 0.2), 0.25, 2.0)
    positions = draw_positions(jax.random.fold_in(streams_of[5], 71), 0)
    return dict(object_tiles=object_tiles, probe=probe, propagator_phase=propagator_phase, measured=measured, positions=positions)


learning_rate = 0.5

def dft_tables(order_size):
    index = jnp.arange(order_size, dtype=jnp.int32)
    product = index[:, None] * index[None, :] % order_size
    angle = product.astype(jnp.float32) * (2.0 * math.pi / order_size)
    factor = 1.0 / math.sqrt(order_size)
    return (jnp.cos(angle) * factor, -jnp.sin(angle) * factor)

def product_left(matrix, operand):
    return jnp.einsum('jk,...kl->...jl', matrix, operand, precision=lax.Precision.HIGHEST)

def product_right(operand, matrix):
    return jnp.einsum('...jk,kl->...jl', operand, matrix, precision=lax.Precision.HIGHEST)

def transform(real_part, imag_part, cos_table, sin_table):
    left_real = product_left(cos_table, real_part) - product_left(sin_table, imag_part)
    left_imag = product_left(cos_table, imag_part) + product_left(sin_table, real_part)
    out_real = product_right(left_real, cos_table) - product_right(left_imag, sin_table)
    out_imag = product_right(left_imag, cos_table) + product_right(left_real, sin_table)
    return (out_real, out_imag)

def multislice(windows, probe, propagator_phase):
    order_size = probe.shape[-1]
    cos_table, sin_table = dft_tables(order_size)
    kernel_cos = jnp.cos(propagator_phase)
    kernel_sin = jnp.sin(propagator_phase)
    wave_real = probe[None, :, 0]
    wave_imag = probe[None, :, 1]
    layers = windows.shape[1]
    for layer_index in range(layers):
        trans_real = 1.0 + windows[:, None, layer_index, 0]
        trans_imag = windows[:, None, layer_index, 1]
        wave_real, wave_imag = (trans_real * wave_real - trans_imag * wave_imag, trans_real * wave_imag + trans_imag * wave_real)
        if layer_index + 1 < layers:
            spec_real, spec_imag = transform(wave_real, wave_imag, cos_table, sin_table)
            spec_real, spec_imag = (kernel_cos * spec_real - kernel_sin * spec_imag, kernel_cos * spec_imag + kernel_sin * spec_real)
            wave_real, wave_imag = transform(spec_real, spec_imag, cos_table, -sin_table)
    return transform(wave_real, wave_imag, cos_table, sin_table)

def windows_of(extended, positions, order_size):
    anchor = jnp.zeros((), jnp.int32)

    def single_window(position):
        starts = (anchor, anchor, position[0].astype(jnp.int32), position[1].astype(jnp.int32))
        return lax.dynamic_slice(extended, starts, (extended.shape[0], 2, order_size, order_size))
    return jax.vmap(single_window)(positions)

def neighbour_piece(tiles, tile_index, row_step, col_step):
    tile_count = tiles.shape[0]
    base = tile_index + row_step * TILE_COLS
    valid = jnp.logical_and(base >= 0, base < tile_count)
    target = jnp.mod(base + col_step, tile_count).astype(jnp.int32)
    piece = lax.dynamic_index_in_dim(tiles, target, 0, keepdims=False)
    core_size = tiles.shape[3]
    if row_step < 0:
        piece = piece[:, :, core_size - HALO:, :]
    elif row_step > 0:
        piece = piece[:, :, :HALO, :]
    if col_step < 0:
        piece = piece[:, :, :, core_size - HALO:]
    elif col_step > 0:
        piece = piece[:, :, :, :HALO]
    return piece * valid.astype(tiles.dtype)

def extend(tiles, tile_index):
    bands = []
    for row_step in (-1, 0, 1):
        band = [neighbour_piece(tiles, tile_index, row_step, col_step) for col_step in (-1, 0, 1)]
        bands.append(jnp.concatenate(band, axis=3))
    return jnp.concatenate(bands, axis=2)

def reference(object_tiles, probe, propagator_phase, measured, positions):
    tile_count = object_tiles.shape[0]
    tile_positions = positions.reshape(tile_count, STEPS, SCANS, 2)
    tile_measured = measured.reshape(tile_count, STEPS, SCANS, K, K)
    tiles = object_tiles
    outputs = []
    for iteration in range(STEPS):

        def tile_step(accumulated, inputs):
            tile_index, these_positions, these_measured = inputs

            def forward_tile(tiles_arg):
                return multislice(windows_of(extend(tiles_arg, tile_index), these_positions, K), probe, propagator_phase)
            (spec_real, spec_imag), pullback = jax.vjp(forward_tile, tiles)
            intensity = lax.optimization_barrier(jnp.sum(spec_real * spec_real + spec_imag * spec_imag, axis=1))
            residual = intensity - these_measured
            gradient, = pullback((2.0 * residual[:, None] * spec_real, 2.0 * residual[:, None] * spec_imag))
            return (accumulated + gradient, intensity)
        gradient, intensities = lax.scan(tile_step, jnp.zeros_like(tiles), (jnp.arange(tile_count, dtype=jnp.int32), tile_positions[:, iteration], tile_measured[:, iteration]))
        tiles = tiles - learning_rate * gradient
        outputs.append(intensities)
    stacked = jnp.stack(outputs, axis=0).transpose(1, 0, 2, 3, 4).reshape(tile_count * STEPS * SCANS, K, K)
    return (tiles, stacked)
```

```python
import functools
import math

import jax
import jax.numpy as jnp
import numpy as np
from jax import lax
from jax.experimental import pallas as pl
from jax.experimental.pallas import tpu as pltpu
from jax.sharding import PartitionSpec as P

K = 128
HALO = 64
EXT = 256
STEPS = 2
TILE_COLS = 8
WAVES = 8

MESH = pl.DeviceIdType.MESH
f32 = jnp.float32
bf16 = jnp.bfloat16


def tables():
    index = np.arange(K)
    angle = (index[:, None] * index[None, :] % K) * (2.0 * math.pi / K)
    cos = np.cos(angle) / math.sqrt(K)
    sin = -np.sin(angle) / math.sqrt(K)
    out = []
    for sign in (1.0, -1.0):
        full = np.block([[cos, sign * sin], [-sign * sin, cos]]).astype(np.float32)
        hi = full.astype(bf16)
        lo = (full - hi.astype(np.float32)).astype(bf16)
        out.append(np.concatenate([hi, lo], axis=0))
    return np.stack(out)


def halves(x):
    return x[:, :K], x[:, K:]


def both(re, im):
    return jnp.concatenate([re, im], axis=1)


def times(x, table):
    hi = x.astype(bf16)
    lo = (x - hi.astype(f32)).astype(bf16)
    return jnp.dot(
        jnp.concatenate([hi, lo, hi], axis=1), table, preferred_element_type=f32
    )


def turned(x):
    re, im = halves(x)
    return both(re.T, im.T)


def mul(a, b):
    ar, ai = a
    br, bi = b
    return ar * br - ai * bi, ar * bi + ai * br


def conj_mul(a, b):
    ar, ai = a
    br, bi = b
    return ar * br + ai * bi, ar * bi - ai * br


def swap_lanes(x):
    return pltpu.roll(x, HALO, axis=1)


def low_lanes(rows):
    return lax.broadcasted_iota(jnp.int32, (rows, K), 1) < HALO


def pack(upper, lower):
    keep = low_lanes(upper.shape[0])
    return (
        jnp.where(keep, upper, swap_lanes(lower)),
        jnp.where(keep, swap_lanes(upper), lower),
    )


def unpack(low, high):
    keep = low_lanes(low.shape[0])
    return (
        jnp.where(keep, low, swap_lanes(high)),
        jnp.where(keep, swap_lanes(low), high),
    )


def kernel(
    pos,
    obj_in,
    probe_in,
    phase_in,
    meas_in,
    table_in,
    obj_out,
    int_out,
    table,
    phase,
    probe,
    meas,
    plane_now,
    wide,
    win_send,
    win,
    psi,
    mid,
    work,
    prop,
    part,
    part_recv,
    inten,
    grad,
    grad_recv,
    placed,
    edge_send,
    edge_recv,
    corner_send,
    corner_recv,
    in_sem,
    out_sem,
    s_probe, r_probe,
    s_win, r_win,
    s_part, r_part,
    s_int, r_int,
    s_grad, r_grad,
    s_edge, r_edge,
    s_corner, r_corner,
    s_fin, r_fin,
):
    tiles = lax.axis_size("tile")
    t = lax.axis_index("tile")
    m = lax.axis_index("mode")
    core = m % 2
    chip = m // 2
    plane = core * 2 + chip

    def tile_at(rows, cols):
        return (lax.rem(t + tiles + rows * TILE_COLS + cols, tiles), m)

    up, down, left, right = tile_at(-1, 0), tile_at(1, 0), tile_at(0, -1), tile_at(0, 1)
    up_left, up_right = tile_at(-1, -1), tile_at(-1, 1)
    down_left, down_right = tile_at(1, -1), tile_at(1, 1)
    mate = [None, m + 1 - 2 * core, lax.rem(m + 2, 4), 3 - m]
    group = [None] + [(t, mate[j]) for j in (1, 2, 3)]

    def plane_of(who):
        return (who % 2) * 2 + who // 2

    def remote(src, dst, send, recv, to):
        return pltpu.make_async_remote_copy(
            src_ref=src, dst_ref=dst, send_sem=send, recv_sem=recv,
            device_id=to, device_id_type=MESH,
        )

    load_obj = pltpu.make_async_copy(obj_in.at[0, core, chip], plane_now, in_sem.at[0])
    load_probe = pltpu.make_async_copy(probe_in, probe.at[pl.ds(0, 4)], in_sem.at[1])
    load_phase = pltpu.make_async_copy(phase_in, phase, in_sem.at[2])
    load_meas = pltpu.make_async_copy(meas_in, meas, in_sem.at[3])
    load_table = pltpu.make_async_copy(table_in, table, in_sem.at[4])
    for copy in (load_obj, load_probe, load_phase, load_meas, load_table):
        copy.start()

    barrier = pltpu.get_barrier_semaphore()
    partners = [up, down, left, right, up_left, up_right, down_left, down_right] + group[1:]
    for who in partners:
        pl.semaphore_signal(barrier, inc=1, device_id=who, device_id_type=MESH)
    load_obj.wait()

    def row_ok():
        row = lax.broadcasted_iota(jnp.int32, (EXT, K), 0)
        first = jnp.where(t >= TILE_COLS, 0, HALO)
        last = jnp.where(t < tiles - TILE_COLS, EXT, EXT - HALO)
        return jnp.logical_and(row >= first, row < last)

    def exchange(e, top, bottom, side_low, side_high, corners, sides):
        low_side, high_side, tl, th, bl, bh = sides
        copies = []
        for i, (block, to) in enumerate(zip(corners, (tl, th, bl, bh))):
            corner_send[e, i] = block
            copies.append(remote(corner_send.at[e, i], corner_recv.at[e, i], s_corner.at[e, i], r_corner.at[e, i], to))
            copies[-1].start()
        for i, (block, to) in enumerate(zip((top, bottom, side_low, side_high), (up, down, low_side, high_side))):
            edge_send[e, i] = block
            copies.append(remote(edge_send.at[e, i], edge_recv.at[e, i], s_edge.at[e, i], r_edge.at[e, i], to))
            copies[-1].start()
        return copies

    def send_edges(e):
        x = plane_now[...]
        side_low, side_high = pack(x[:HALO], x[HALO:])
        t_low, t_high = pack(x[:32], x[32:64])
        b_low, b_high = pack(x[64:96], x[96:])
        return exchange(
            e, x[:HALO], x[HALO:], side_low, side_high, (t_low, t_high, b_low, b_high),
            (left, right, up_left, up_right, down_left, down_right),
        )

    def take_edges(e, copies):
        wide[0, HALO : HALO + K] = plane_now[...]
        for copy in copies:
            copy.wait()
        first = jnp.where(t >= TILE_COLS, 1.0, 0.0)
        last = jnp.where(t < tiles - TILE_COLS, 1.0, 0.0)
        wide[0, HALO + K :] = edge_recv[e, 0] * last
        wide[0, :HALO] = edge_recv[e, 1] * first
        a, b = unpack(edge_recv[e, 2], edge_recv[e, 3])
        wide[1, HALO:K] = a
        wide[1, K : K + HALO] = b
        a, b = unpack(corner_recv[e, 0], corner_recv[e, 1])
        wide[1, 192:224] = a * last
        wide[1, 224:256] = b * last
        a, b = unpack(corner_recv[e, 2], corner_recv[e, 3])
        wide[1, 0:32] = a * first
        wide[1, 32:64] = b * first

    def fold(e, inner, outer):
        side_low, side_high = pack(outer[HALO:K], outer[K : K + HALO])
        t_low, t_high = pack(outer[0:32], outer[32:64])
        b_low, b_high = pack(outer[192:224], outer[224:256])
        copies = exchange(
            e, inner[:HALO], inner[K + HALO :], side_low, side_high, (t_low, t_high, b_low, b_high),
            (right, left, up_right, up_left, down_right, down_left),
        )
        for copy in copies:
            copy.wait()
        a, b = unpack(edge_recv[e, 2], edge_recv[e, 3])
        top = inner[HALO:K] + edge_recv[e, 1] + a
        bottom = inner[K : K + HALO] + edge_recv[e, 0] + b
        ta, tb = unpack(corner_recv[e, 2], corner_recv[e, 3])
        ba, bb = unpack(corner_recv[e, 0], corner_recv[e, 1])
        top = top + jnp.concatenate([ta, tb], axis=0)
        bottom = bottom + jnp.concatenate([ba, bb], axis=0)
        return jnp.concatenate([top, bottom], axis=0)

    def window(n, q):
        r = pos[n * 2 + q, 0]
        c = pos[n * 2 + q, 1]
        rows = both(wide[0, pl.ds(r, K), :], wide[1, pl.ds(r, K), :])
        return pltpu.roll(rows, lax.rem(EXT + HALO - c, EXT), axis=1)[:, :K]

    def send_windows(n):
        copies = [
            remote(win_send.at[n, 0], win.at[n, plane], s_win.at[n, 0], r_win.at[n, 0], group[1]),
            remote(win_send.at[n, 1], win.at[n, plane], s_win.at[n, 1], r_win.at[n, 1], group[2]),
            remote(win_send.at[n, 1], win.at[n, plane], s_win.at[n, 2], r_win.at[n, 2], group[3]),
        ]
        win_send[n, 1] = window(n, 1 - chip)
        copies[1].start()
        copies[2].start()
        own = window(n, chip)
        win_send[n, 0] = own
        copies[0].start()
        win[n, plane] = own
        return copies

    def place(n, q, g):
        r = pos[n * 2 + q, 0]
        c = pos[n * 2 + q, 1]
        padded = both(g, jnp.zeros((K, K), f32))
        a, b = halves(pltpu.roll(padded, lax.rem(c + EXT - HALO, EXT), axis=1))
        placed[0, K : 2 * K] = a
        placed[1, K : 2 * K] = b
        rows = pl.ds(K - r, EXT)
        return placed[0, rows, :], placed[1, rows, :]

    def tab(which):
        hi = table[which, 0:EXT]
        return jnp.concatenate([hi, hi, table[which, EXT:]], axis=0)

    pl.semaphore_wait(barrier, len(partners))
    send_probe = remote(probe.at[pl.ds(0, 4)], probe.at[pl.ds(4, 4)], s_probe.at[0], r_probe.at[0], group[2])
    pending = []
    halo_copies = send_edges(0)
    load_probe.wait()
    send_probe.start()
    load_phase.wait()
    angle = phase[...].T
    prop[0] = jnp.cos(angle)
    prop[1] = jnp.sin(angle)
    for half in range(2):
        placed[half] = jnp.zeros((384, K), f32)
    take_edges(0, halo_copies)
    win_copies = send_windows(0)
    load_meas.wait()
    load_table.wait()

    for n in range(STEPS):
        meas_n = meas[n * 2 + chip].T

        def f1(j):
            re, im = mul((1.0 + win[n, 0], win[n, 1]), (probe[j, 0], probe[j, 1]))
            work[j] = turned(times(both(re, im), tab(0)))

        def f2(j):
            y = halves(times(work[j], tab(0)))
            work[j] = both(*mul((prop[0], prop[1]), y))

        def f3(j):
            work[j] = turned(times(work[j], tab(1)))

        def f4(j):
            y = times(work[j], tab(1))
            mid[j] = y
            work[j] = both(*mul((1.0 + win[n, 2], win[n, 3]), halves(y)))

        def f5(j):
            work[j] = turned(times(work[j], tab(0)))

        def f6(j):
            y = times(work[j], tab(0))
            psi[j] = y
            re, im = halves(y)
            if j == 0:
                part[n] = re * re + im * im
            else:
                part[n] += re * re + im * im

        for copy in win_copies:
            copy.wait()
        groups = ((0, 1, 2, 3), (4, 5, 6, 7)) if n == 0 else (range(WAVES),)
        for g, waves in enumerate(groups):
            if n == 0 and g == 1:
                send_probe.wait()
            for stage in (f1, f2, f3, f4, f5, f6):
                for j in waves:
                    stage(j)

        send_part = remote(part.at[n], part_recv.at[n], s_part.at[n], r_part.at[n], group[1])
        send_part.start()
        send_part.wait()
        intensity = part[n] + part_recv[n]
        residual = intensity - meas_n
        inten[n] = intensity.T

        def b1(j):
            work[j] = turned(times(both(residual, residual) * psi[j], tab(1)))

        def b2(j):
            g = halves(times(work[j], tab(1)))
            re, im = conj_mul(halves(mid[j]), g)
            if j == 0:
                grad[n, 2] = re
                grad[n, 3] = im
            else:
                grad[n, 2] += re
                grad[n, 3] += im
            work[j] = both(*conj_mul((1.0 + win[n, 2], win[n, 3]), g))

        def b3(j):
            work[j] = turned(times(work[j], tab(0)))

        def b4(j):
            y = halves(times(work[j], tab(0)))
            work[j] = both(*conj_mul((prop[0], prop[1]), y))

        def b5(j):
            work[j] = turned(times(work[j], tab(1)))

        def b6(j):
            g = halves(times(work[j], tab(1)))
            re, im = conj_mul((probe[j, 0], probe[j, 1]), g)
            if j == 0:
                grad[n, 0] = re
                grad[n, 1] = im
            else:
                grad[n, 0] += re
                grad[n, 1] += im

        grad_copies = [
            remote(
                grad.at[n, plane_of(mate[j])], grad_recv.at[n, j - 1],
                s_grad.at[n, j - 1], r_grad.at[n, j - 1], group[j],
            )
            for j in (1, 2, 3)
        ]

        for stage in (b1, b2):
            for j in range(WAVES):
                stage(j)

        @pl.when(core == 1)
        def _():
            grad_copies[1].start()

        @pl.when(core == 0)
        def _():
            grad_copies[2].start()
            grad_copies[0].start()

        for stage in (b3, b4, b5, b6):
            for j in range(WAVES):
                stage(j)

        @pl.when(core == 0)
        def _():
            grad_copies[1].start()

        @pl.when(core == 1)
        def _():
            grad_copies[2].start()
            grad_copies[0].start()

        slot = n * 2 + chip
        keep_int = pltpu.make_async_copy(inten.at[n], int_out.at[slot], out_sem.at[n])
        send_int = remote(inten.at[n], int_out.at[slot], s_int.at[n], r_int.at[n], group[2])

        for copy in grad_copies:
            copy.wait()
        inner, outer = place(n, chip, grad[n, plane] + grad_recv[n, 0])
        inner2, outer2 = place(n, 1 - chip, grad_recv[n, 1] + grad_recv[n, 2])
        ok = row_ok()
        inner = jnp.where(ok, inner + inner2, 0.0)
        outer = jnp.where(ok, outer + outer2, 0.0)
        keep_int.start()
        total = fold(1 + 2 * n, inner, outer)
        send_int.start()
        pending += [keep_int, send_int]
        plane_now[...] = plane_now[...] - total
        if n + 1 < STEPS:
            take_edges(2 + 2 * n, send_edges(2 + 2 * n))
            win_copies = send_windows(n + 1)

    there = obj_out.at[0, core, chip]
    for j in (3, 2, 1):
        copy = remote(plane_now, there, s_fin.at[j - 1], r_fin.at[j - 1], group[j])
        copy.start()
        pending.append(copy)
    keep_obj = pltpu.make_async_copy(plane_now, there, out_sem.at[2])
    keep_obj.start()
    pending.append(keep_obj)
    for copy in pending:
        copy.wait()


def local(object_tiles, probe, propagator_phase, measured, positions):
    anywhere = pl.BlockSpec(memory_space=pl.ANY)
    dma = pltpu.SemaphoreType.DMA
    V = pltpu.VMEM
    scratch = [
        V((2, 2 * EXT, EXT), bf16),
        V((K, K), f32),
        V((WAVES, 2, K, K), f32),
        V((4, K, K), f32),
        V((K, K), f32),
        V((2, EXT, K), f32),
        V((2, 2, K, K), f32),
        V((2, 4, K, K), f32),
        V((WAVES, K, EXT), f32),
        V((WAVES, K, EXT), f32),
        V((WAVES, K, EXT), f32),
        V((2, K, K), f32),
        V((2, K, K), f32),
        V((2, K, K), f32),
        V((2, K, K), f32),
        V((2, 4, K, K), f32),
        V((2, 3, K, K), f32),
        V((2, 384, K), f32),
        V((4, 4, HALO, K), f32),
        V((4, 4, HALO, K), f32),
        V((4, 4, 32, K), f32),
        V((4, 4, 32, K), f32),
        dma((5,)),
        dma((3,)),
        dma((1,)), dma((1,)),
        dma((2, 3)), dma((2, 3)),
        dma((2,)), dma((2,)),
        dma((2,)), dma((2,)),
        dma((2, 3)), dma((2, 3)),
        dma((4, 4)), dma((4, 4)),
        dma((4, 4)), dma((4, 4)),
        dma((3,)), dma((3,)),
    ]
    return pl.pallas_call(
        kernel,
        name="ptycho",
        out_shape=(
            jax.ShapeDtypeStruct(object_tiles.shape, f32),
            jax.ShapeDtypeStruct(measured.shape, f32),
        ),
        in_specs=[pl.BlockSpec(memory_space=pltpu.SMEM)] + [anywhere] * 5,
        out_specs=(anywhere, anywhere),
        scratch_shapes=scratch,
        compiler_params=pltpu.CompilerParams(
            collective_id=0, has_side_effects=True, vmem_limit_bytes=48 * 1024 * 1024
        ),
    )(positions, object_tiles, probe, propagator_phase, measured, jnp.asarray(tables()))


def solution(mesh):
    return jax.shard_map(
        local,
        mesh=mesh,
        in_specs=(
            P("tile", None, None, None, None),
            P("mode", None, None, None),
            P(),
            P("tile", None, None),
            P("tile", None),
        ),
        out_specs=(P("tile", None, None, None, None), P("tile", None, None)),
        check_vma=False,
    )
```

```python
import functools
import math

import jax
import jax.numpy as jnp
import numpy as np
from jax import lax
from jax.experimental import pallas as pl
from jax.experimental.pallas import tpu as pltpu
from jax.sharding import PartitionSpec as P

K = 128
HALO = 64
EXT = 256
STEPS = 2
TILE_COLS = 8
WAVES = 8

MESH = pl.DeviceIdType.MESH
f32 = jnp.float32
bf16 = jnp.bfloat16


def tables():
    index = np.arange(K)
    angle = (index[:, None] * index[None, :] % K) * (2.0 * math.pi / K)
    cos = np.cos(angle) / math.sqrt(K)
    sin = -np.sin(angle) / math.sqrt(K)
    out = []
    for sign in (1.0, -1.0):
        full = np.block([[cos, sign * sin], [-sign * sin, cos]]).astype(np.float32)
        hi = full.astype(bf16)
        lo = (full - hi.astype(np.float32)).astype(bf16)
        out.append(np.concatenate([hi, lo], axis=0))
    return np.stack(out)


def halves(x):
    return x[:, :K], x[:, K:]


def both(re, im):
    return jnp.concatenate([re, im], axis=1)


def times(x, table):
    hi = x.astype(bf16)
    lo = (x - hi.astype(f32)).astype(bf16)
    return jnp.dot(
        jnp.concatenate([hi, lo, hi], axis=1), table, preferred_element_type=f32
    )


def turned(x):
    re, im = halves(x)
    return both(re.T, im.T)


def mul(a, b):
    ar, ai = a
    br, bi = b
    return ar * br - ai * bi, ar * bi + ai * br


def conj_mul(a, b):
    ar, ai = a
    br, bi = b
    return ar * br + ai * bi, ar * bi - ai * br


def swap_lanes(x):
    return pltpu.roll(x, HALO, axis=1)


def low_lanes(rows):
    return lax.broadcasted_iota(jnp.int32, (rows, K), 1) < HALO


def pack(upper, lower):
    keep = low_lanes(upper.shape[0])
    return (
        jnp.where(keep, upper, swap_lanes(lower)),
        jnp.where(keep, swap_lanes(upper), lower),
    )


def unpack(low, high):
    keep = low_lanes(low.shape[0])
    return (
        jnp.where(keep, low, swap_lanes(high)),
        jnp.where(keep, swap_lanes(low), high),
    )


def kernel(
    pos,
    obj_in,
    probe_in,
    phase_in,
    meas_in,
    table_in,
    obj_out,
    int_out,
    table,
    phase,
    probe,
    meas,
    plane_now,
    wide,
    win_send,
    win,
    psi,
    mid,
    work,
    prop,
    part,
    part_recv,
    inten,
    grad,
    grad_recv,
    placed,
    edge_send,
    edge_recv,
    corner_send,
    corner_recv,
    in_sem,
    out_sem,
    s_probe, r_probe,
    s_win, r_win,
    s_part, r_part,
    s_int, r_int,
    s_grad, r_grad,
    s_edge, r_edge,
    s_corner, r_corner,
    s_fin, r_fin,
):
    tiles = lax.axis_size("tile")
    t = lax.axis_index("tile")
    m = lax.axis_index("mode")
    core = m % 2
    chip = m // 2
    comp = (chip + t // TILE_COLS) % 2
    plane = core * 2 + comp
    pattern = [core, chip]
    same = [2, 1]
    swap = [1, 2]

    def tile_at(rows, cols):
        there = lax.rem(t + tiles + rows * TILE_COLS + cols, tiles)
        return (there, (comp + there // TILE_COLS) % 2 * 2 + core)

    up, down, left, right = tile_at(-1, 0), tile_at(1, 0), tile_at(0, -1), tile_at(0, 1)
    up_left, up_right = tile_at(-1, -1), tile_at(-1, 1)
    down_left, down_right = tile_at(1, -1), tile_at(1, 1)
    mate = [None, m + 1 - 2 * core, lax.rem(m + 2, 4), 3 - m]
    group = [None] + [(t, mate[j]) for j in (1, 2, 3)]

    def plane_of(who):
        return (who % 2) * 2 + (who // 2 + t // TILE_COLS) % 2

    def remote(src, dst, send, recv, to):
        return pltpu.make_async_remote_copy(
            src_ref=src, dst_ref=dst, send_sem=send, recv_sem=recv,
            device_id=to, device_id_type=MESH,
        )

    load_plane = pltpu.make_async_copy(obj_in.at[0, core, comp], plane_now, in_sem.at[0])
    load_probe = pltpu.make_async_copy(probe_in, probe.at[pl.ds(0, 4)], in_sem.at[1])
    load_phase = pltpu.make_async_copy(phase_in, phase, in_sem.at[2])
    load_meas = pltpu.make_async_copy(meas_in, meas, in_sem.at[3])
    load_table = pltpu.make_async_copy(table_in, table, in_sem.at[4])
    for copy in (load_plane, load_probe, load_phase, load_meas, load_table):
        copy.start()

    barrier = pltpu.get_barrier_semaphore()
    partners = [up, down, left, right, up_left, up_right, down_left, down_right] + group[1:]
    for who in partners:
        pl.semaphore_signal(barrier, inc=1, device_id=who, device_id_type=MESH)

    def row_ok():
        row = lax.broadcasted_iota(jnp.int32, (EXT, K), 0)
        first = jnp.where(t >= TILE_COLS, 0, HALO)
        last = jnp.where(t < tiles - TILE_COLS, EXT, EXT - HALO)
        return jnp.logical_and(row >= first, row < last)

    def exchange(e, top, bottom, side_low, side_high, corners, sides):
        low_side, high_side, tl, th, bl, bh = sides
        copies = []
        for i, (block, to) in enumerate(zip(corners, (tl, th, bl, bh))):
            corner_send[e, i] = block
            copies.append(remote(corner_send.at[e, i], corner_recv.at[e, i], s_corner.at[e, i], r_corner.at[e, i], to))
            copies[-1].start()
        for i, (block, to) in enumerate(zip((top, bottom, side_low, side_high), (up, down, low_side, high_side))):
            edge_send[e, i] = block
            copies.append(remote(edge_send.at[e, i], edge_recv.at[e, i], s_edge.at[e, i], r_edge.at[e, i], to))
            copies[-1].start()
        return copies

    def arrived(copies):
        for copy in copies:
            copy.wait_recv()
        sent.extend(copies)

    def send_edges(e, x):
        side_low, side_high = pack(x[:HALO], x[HALO:])
        t_low, t_high = pack(x[:32], x[32:64])
        b_low, b_high = pack(x[64:96], x[96:])
        return exchange(
            e, x[:HALO], x[HALO:], side_low, side_high, (t_low, t_high, b_low, b_high),
            (left, right, up_left, up_right, down_left, down_right),
        )

    def take_edges(e, x, copies):
        wide[0, HALO : HALO + K] = x
        first = jnp.where(t >= TILE_COLS, 1.0, 0.0)
        last = jnp.where(t < tiles - TILE_COLS, 1.0, 0.0)
        arrived(copies[6:])
        a, b = unpack(edge_recv[e, 2], edge_recv[e, 3])
        wide[1, HALO:K] = a
        wide[1, K : K + HALO] = b
        arrived(copies[4:6])
        wide[0, HALO + K :] = edge_recv[e, 0] * last
        wide[0, :HALO] = edge_recv[e, 1] * first
        arrived(copies[:4])
        a, b = unpack(corner_recv[e, 0], corner_recv[e, 1])
        wide[1, 192:224] = a * last
        wide[1, 224:256] = b * last
        a, b = unpack(corner_recv[e, 2], corner_recv[e, 3])
        wide[1, 0:32] = a * first
        wide[1, 32:64] = b * first

    def fold(e, inner, outer, after=()):
        side_low, side_high = pack(outer[HALO:K], outer[K : K + HALO])
        t_low, t_high = pack(outer[0:32], outer[32:64])
        b_low, b_high = pack(outer[192:224], outer[224:256])
        copies = exchange(
            e, inner[:HALO], inner[K + HALO :], side_low, side_high, (t_low, t_high, b_low, b_high),
            (right, left, up_right, up_left, down_right, down_left),
        )
        for copy in after:
            copy.start()
        arrived(copies[6:])
        a, b = unpack(edge_recv[e, 2], edge_recv[e, 3])
        arrived(copies[4:6])
        top = inner[HALO:K] + edge_recv[e, 1] + a
        bottom = inner[K : K + HALO] + edge_recv[e, 0] + b
        arrived(copies[:4])
        ta, tb = unpack(corner_recv[e, 2], corner_recv[e, 3])
        ba, bb = unpack(corner_recv[e, 0], corner_recv[e, 1])
        top = top + jnp.concatenate([ta, tb], axis=0)
        bottom = bottom + jnp.concatenate([ba, bb], axis=0)
        return jnp.concatenate([top, bottom], axis=0)

    def window(n, q):
        r = pos[0, n * 2 + q]
        c = pos[1, n * 2 + q]
        rows = both(wide[0, pl.ds(r, K), :], wide[1, pl.ds(r, K), :])
        return pltpu.roll(rows, lax.rem(EXT + HALO - c, EXT), axis=1)[:, :K]

    def send_windows(n):
        copies = [
            remote(
                win_send.at[n, 0 if j == same[n] else 1], win.at[n, plane],
                s_win.at[n, j - 1], r_win.at[n, j - 1], group[j],
            )
            for j in (1, 2, 3)
        ]
        own = window(n, pattern[n])
        if same[n] == 2:
            win_send[n, 0] = own
            copies[1].start()
        win_send[n, 1] = window(n, 1 - pattern[n])
        copies[2].start()
        copies[swap[n] - 1].start()
        if same[n] == 1:
            win_send[n, 0] = own
            copies[0].start()
        win[n, plane] = own
        return copies

    def place(n, q, g):
        r = pos[0, n * 2 + q]
        c = pos[1, n * 2 + q]
        padded = both(g, jnp.zeros((K, K), f32))
        a, b = halves(pltpu.roll(padded, lax.rem(c + EXT - HALO, EXT), axis=1))
        placed[0, K : 2 * K] = a
        placed[1, K : 2 * K] = b
        rows = pl.ds(K - r, EXT)
        return placed[0, rows, :], placed[1, rows, :]

    def tab(which):
        hi = table[which, 0:EXT]
        return jnp.concatenate([hi, hi, table[which, EXT:]], axis=0)

    pl.semaphore_wait(barrier, len(partners))
    probe_copies = [
        remote(probe.at[pl.ds(0, 4)], probe.at[pl.ds(4, 4)], s_probe.at[0], r_probe.at[0], group[1]),
    ] + [
        remote(probe.at[i], probe.at[8 + i], s_probe.at[1 + i], r_probe.at[1 + i], group[2])
        for i in range(4)
    ]
    sent = []
    pending = []
    load_plane.wait()
    first_copies = send_edges(0, plane_now[...])
    load_probe.wait()
    probe_copies[0].start()
    load_phase.wait()
    angle = phase[...].T
    prop[0] = jnp.cos(angle)
    prop[1] = jnp.sin(angle)
    for half in range(2):
        placed[half] = jnp.zeros((384, K), f32)
    load_meas.wait()
    load_table.wait()
    take_edges(0, plane_now[...], first_copies)
    win_copies = send_windows(0)

    for n in range(STEPS):
        meas_n = meas[n * 2 + pattern[n]].T

        def mode(j):
            at = j if n == 0 or j < 4 else j + 4
            return probe[at, 0], probe[at, 1]

        def wait_windows(n, s):
            @pl.when(core == s)
            def _():
                win_copies[1].wait_recv()

            @pl.when(core != s)
            def _():
                win_copies[0].wait_recv()
                win_copies[2].wait_recv()

            if s == 1:
                sent.extend(win_copies)

        def f1(j):
            re, im = mul((1.0 + win[n, 0], win[n, 1]), mode(j))
            work[j] = turned(times(both(re, im), tab(0)))

        def f2(j):
            y = halves(times(work[j], tab(0)))
            work[j] = both(*mul((prop[0], prop[1]), y))

        def f3(j):
            work[j] = turned(times(work[j], tab(1)))

        def f4(j):
            y = times(work[j], tab(1))
            mid[j] = y
            work[j] = both(*mul((1.0 + win[n, 2], win[n, 3]), halves(y)))

        def f5(j):
            work[j] = turned(times(work[j], tab(0)))

        def f6(j):
            y = times(work[j], tab(0))
            psi[j] = y
            re, im = halves(y)
            if j == 0:
                part[n] = re * re + im * im
            else:
                part[n] += re * re + im * im

        if n == 0:
            probe_copies[1].start()
        arrived(probe_copies[1:] if n else probe_copies[:1])
        for stage in (f1, f2, f3, f4, f5, f6):
            if stage is f1:
                wait_windows(n, 0)
            if stage is f4:
                wait_windows(n, 1)
            for j in range(WAVES):
                stage(j)

        send_part = remote(part.at[n], part_recv.at[n], s_part.at[n], r_part.at[n], group[same[n]])
        send_part.start()
        arrived([send_part])
        if n == 0:
            probe_copies[2].start()
        intensity = part[n] + part_recv[n]
        residual = intensity - meas_n
        inten[n] = intensity.T

        def b1(j):
            work[j] = turned(times(both(residual, residual) * psi[j], tab(1)))

        def b2(j):
            g = halves(times(work[j], tab(1)))
            re, im = conj_mul(halves(mid[j]), g)
            if j == 0:
                grad[n, 2] = re
                grad[n, 3] = im
            else:
                grad[n, 2] += re
                grad[n, 3] += im
            work[j] = both(*conj_mul((1.0 + win[n, 2], win[n, 3]), g))

        def b3(j):
            work[j] = turned(times(work[j], tab(0)))

        def b4(j):
            y = halves(times(work[j], tab(0)))
            work[j] = both(*conj_mul((prop[0], prop[1]), y))

        def b5(j):
            work[j] = turned(times(work[j], tab(1)))

        def b6(j):
            g = halves(times(work[j], tab(1)))
            re, im = conj_mul(mode(j), g)
            if j == 0:
                grad[n, 0] = re
                grad[n, 1] = im
            else:
                grad[n, 0] += re
                grad[n, 1] += im

        grad_copies = [
            remote(
                grad.at[n, plane_of(mate[j])], grad_recv.at[n, j - 1],
                s_grad.at[n, j - 1], r_grad.at[n, j - 1], group[j],
            )
            for j in (1, 2, 3)
        ]

        for stage in (b1, b2):
            for j in range(WAVES):
                stage(j)

        @pl.when(core == 1)
        def _():
            grad_copies[1].start()

        @pl.when(core == 0)
        def _():
            grad_copies[2].start()
            grad_copies[0].start()

        for stage in (b3, b4, b5, b6):
            for j in range(WAVES):
                stage(j)

        @pl.when(core == 0)
        def _():
            grad_copies[1].start()

        @pl.when(core == 1)
        def _():
            grad_copies[2].start()
            grad_copies[0].start()

        slot = n * 2 + pattern[n]
        keep_int = pltpu.make_async_copy(inten.at[n], int_out.at[slot], out_sem.at[n])
        send_int = remote(inten.at[n], int_out.at[slot], s_int.at[n], r_int.at[n], group[swap[n]])

        a, b = same[n] - 1, swap[n] - 1
        arrived([grad_copies[0], grad_copies[a]] if a else [grad_copies[0]])
        inner, outer = place(n, pattern[n], grad[n, plane] + grad_recv[n, a])
        arrived([grad_copies[2]] if a else grad_copies[1:])
        inner2, outer2 = place(n, 1 - pattern[n], grad_recv[n, b] + grad_recv[n, 2])
        ok = row_ok()
        inner = jnp.where(ok, inner + inner2, 0.0)
        outer = jnp.where(ok, outer + outer2, 0.0)
        keep_int.start()
        total = fold(1 + 2 * n, inner, outer, probe_copies[3 + n : 4 + n] if n == 0 else [])
        send_int.start()
        pending += [keep_int, send_int]
        plane_now[...] = plane_now[...] - total
        if n + 1 < STEPS:
            x = plane_now[...]
            edges = send_edges(2 + 2 * n, x)
            probe_copies[4].start()
            take_edges(2 + 2 * n, x, edges)
            win_copies = send_windows(n + 1)

    there = obj_out.at[0, core, comp]
    for j in (3, 2, 1):
        copy = remote(plane_now, there, s_fin.at[j - 1], r_fin.at[j - 1], group[j])
        copy.start()
        pending.append(copy)
    keep_obj = pltpu.make_async_copy(plane_now, there, out_sem.at[2])
    keep_obj.start()
    pending.append(keep_obj)
    for copy in sent:
        copy.wait_send()
    for copy in pending:
        copy.wait()


def local(object_tiles, probe, propagator_phase, measured, positions):
    anywhere = pl.BlockSpec(memory_space=pl.ANY)
    dma = pltpu.SemaphoreType.DMA
    V = pltpu.VMEM
    scratch = [
        V((2, 2 * EXT, EXT), bf16),
        V((K, K), f32),
        V((12, 2, K, K), f32),
        V((4, K, K), f32),
        V((K, K), f32),
        V((2, EXT, K), f32),
        V((2, 2, K, K), f32),
        V((2, 4, K, K), f32),
        V((WAVES, K, EXT), f32),
        V((WAVES, K, EXT), f32),
        V((WAVES, K, EXT), f32),
        V((2, K, K), f32),
        V((2, K, K), f32),
        V((2, K, K), f32),
        V((2, K, K), f32),
        V((2, 4, K, K), f32),
        V((2, 3, K, K), f32),
        V((2, 384, K), f32),
        V((4, 4, HALO, K), f32),
        V((4, 4, HALO, K), f32),
        V((4, 4, 32, K), f32),
        V((4, 4, 32, K), f32),
        dma((5,)),
        dma((3,)),
        dma((5,)), dma((5,)),
        dma((2, 3)), dma((2, 3)),
        dma((2,)), dma((2,)),
        dma((2,)), dma((2,)),
        dma((2, 3)), dma((2, 3)),
        dma((4, 4)), dma((4, 4)),
        dma((4, 4)), dma((4, 4)),
        dma((3,)), dma((3,)),
    ]
    outs = pl.pallas_call(
        kernel,
        name="ptycho",
        out_shape=(
            jax.ShapeDtypeStruct(object_tiles.shape, f32),
            jax.ShapeDtypeStruct(measured.shape, f32),
        ),
        in_specs=[pl.BlockSpec(memory_space=pltpu.SMEM)] + [anywhere] * 5,
        out_specs=(anywhere, anywhere),
        scratch_shapes=scratch,
        compiler_params=pltpu.CompilerParams(
            collective_id=0, has_side_effects=True
        ),
    )(positions.T, object_tiles, probe, propagator_phase, measured, jnp.asarray(tables()))
    return pl.pallas_call(
        hand_over,
        name="hand_over",
        out_shape=tuple(jax.ShapeDtypeStruct(x.shape, f32) for x in outs),
        in_specs=[anywhere] * 2,
        out_specs=(anywhere, anywhere),
        scratch_shapes=[V(x.shape, f32) for x in outs] + [dma((2,)), dma((2,))],
    )(*outs)


def hand_over(obj_in, int_in, obj_out, int_out, obj, inten, in_sem, out_sem):
    ins = [
        pltpu.make_async_copy(obj_in, obj, in_sem.at[0]),
        pltpu.make_async_copy(int_in, inten, in_sem.at[1]),
    ]
    outs = [
        pltpu.make_async_copy(obj, obj_out, out_sem.at[0]),
        pltpu.make_async_copy(inten, int_out, out_sem.at[1]),
    ]
    for copy in ins:
        copy.start()
    for copy, out in zip(ins, outs):
        copy.wait()
        out.start()
    for out in outs:
        out.wait()


def solution(mesh):
    return jax.shard_map(
        local,
        mesh=mesh,
        in_specs=(
            P("tile", None, None, None, None),
            P("mode", None, None, None),
            P(),
            P("tile", None, None),
            P("tile", None),
        ),
        out_specs=(P("tile", None, None, None, None), P("tile", None, None)),
        check_vma=False,
    )
```

```python
import functools
import math

import jax
import jax.numpy as jnp
import numpy as np
from jax import lax
from jax.experimental import pallas as pl
from jax.experimental.pallas import tpu as pltpu
from jax.sharding import PartitionSpec as P

K = 128
HALO = 64
EXT = 256
STEPS = 2
TILE_COLS = 8
WAVES = 8
SEND_ORDER = (0, 3, 1, 2, 4, 5, 6, 7)

MESH = pl.DeviceIdType.MESH
f32 = jnp.float32
bf16 = jnp.bfloat16


def tables():
    index = np.arange(K)
    angle = (index[:, None] * index[None, :] % K) * (2.0 * math.pi / K)
    cos = np.cos(angle) / math.sqrt(K)
    sin = -np.sin(angle) / math.sqrt(K)
    out = []
    for sign in (1.0, -1.0):
        full = np.block([[cos, sign * sin], [-sign * sin, cos]]).astype(np.float32)
        hi = full.astype(bf16)
        lo = (full - hi.astype(np.float32)).astype(bf16)
        out.append(np.concatenate([hi, lo], axis=0))
    return np.stack(out)


def halves(x):
    return x[:, :K], x[:, K:]


def both(re, im):
    return jnp.concatenate([re, im], axis=1)


def times(x, table):
    hi = x.astype(bf16)
    lo = (x - hi.astype(f32)).astype(bf16)
    return jnp.dot(
        jnp.concatenate([hi, lo, hi], axis=1), table, preferred_element_type=f32
    )


def turned(x):
    re, im = halves(x)
    return both(re.T, im.T)


def mul(a, b):
    ar, ai = a
    br, bi = b
    return ar * br - ai * bi, ar * bi + ai * br


def conj_mul(a, b):
    ar, ai = a
    br, bi = b
    return ar * br + ai * bi, ar * bi - ai * br


def swap_lanes(x):
    return pltpu.roll(x, HALO, axis=1)


def low_lanes(rows):
    return lax.broadcasted_iota(jnp.int32, (rows, K), 1) < HALO


def pack(upper, lower):
    keep = low_lanes(upper.shape[0])
    return (
        jnp.where(keep, upper, swap_lanes(lower)),
        jnp.where(keep, swap_lanes(upper), lower),
    )


def unpack(low, high):
    keep = low_lanes(low.shape[0])
    return (
        jnp.where(keep, low, swap_lanes(high)),
        jnp.where(keep, swap_lanes(low), high),
    )


def kernel(
    pos_in,
    obj_in,
    probe_in,
    phase_in,
    meas_in,
    table_in,
    obj_out,
    int_out,
    pos,
    table,
    phase,
    probe,
    meas,
    plane_now,
    wide,
    win_send,
    win,
    psi,
    mid,
    work,
    prop,
    part,
    part_recv,
    inten,
    grad,
    grad_recv,
    placed,
    edge_send,
    edge_recv,
    corner_send,
    corner_recv,
    in_sem,
    out_sem,
    s_probe, r_probe,
    s_win, r_win,
    s_part, r_part,
    s_int, r_int,
    s_grad, r_grad,
    s_edge, r_edge,
    s_corner, r_corner,
    s_fin, r_fin,
):
    tiles = lax.axis_size("tile")
    t = lax.axis_index("tile")
    m = lax.axis_index("mode")
    core = m % 2
    chip = m // 2
    comp = (chip + t // TILE_COLS) % 2
    plane = core * 2 + comp
    pattern = [core, chip]
    same = [2, 1]
    swap = [1, 2]

    def tile_at(rows, cols):
        there = lax.rem(t + tiles + rows * TILE_COLS + cols, tiles)
        return (there, (comp + there // TILE_COLS) % 2 * 2 + core)

    up, down, left, right = tile_at(-1, 0), tile_at(1, 0), tile_at(0, -1), tile_at(0, 1)
    up_left, up_right = tile_at(-1, -1), tile_at(-1, 1)
    down_left, down_right = tile_at(1, -1), tile_at(1, 1)
    mate = [None, m + 1 - 2 * core, lax.rem(m + 2, 4), 3 - m]
    group = [None] + [(t, mate[j]) for j in (1, 2, 3)]

    def plane_of(who):
        return (who % 2) * 2 + (who // 2 + t // TILE_COLS) % 2

    def remote(src, dst, send, recv, to):
        return pltpu.make_async_remote_copy(
            src_ref=src, dst_ref=dst, send_sem=send, recv_sem=recv,
            device_id=to, device_id_type=MESH,
        )

    barrier = pltpu.get_barrier_semaphore()
    partners = [up, down, left, right, up_left, up_right, down_left, down_right] + group[1:]
    for who in partners:
        pl.semaphore_signal(barrier, inc=1, device_id=who, device_id_type=MESH)

    load_plane = pltpu.make_async_copy(obj_in.at[0, core, comp], plane_now, in_sem.at[0])
    load_probe = pltpu.make_async_copy(probe_in, probe.at[pl.ds(0, 4)], in_sem.at[1])
    load_phase = pltpu.make_async_copy(phase_in, phase, in_sem.at[2])
    load_meas = pltpu.make_async_copy(meas_in, meas, in_sem.at[3])
    load_table = pltpu.make_async_copy(table_in, table, in_sem.at[4])
    load_pos = pltpu.make_async_copy(pos_in, pos, in_sem.at[5])
    for copy in (load_plane, load_pos, load_probe, load_phase, load_meas, load_table):
        copy.start()

    def row_ok():
        row = lax.broadcasted_iota(jnp.int32, (EXT, K), 0)
        first = jnp.where(t >= TILE_COLS, 0, HALO)
        last = jnp.where(t < tiles - TILE_COLS, EXT, EXT - HALO)
        return jnp.logical_and(row >= first, row < last)

    def exchange(e, top, bottom, side_low, side_high, corners, sides):
        low_side, high_side, tl, th, bl, bh = sides
        copies = []
        for i, (block, to) in enumerate(zip(corners, (tl, th, bl, bh))):
            corner_send[e, i] = block
            copies.append(remote(corner_send.at[e, i], corner_recv.at[e, i], s_corner.at[e, i], r_corner.at[e, i], to))
        for i, (block, to) in enumerate(zip((top, bottom, side_low, side_high), (up, down, low_side, high_side))):
            edge_send[e, i] = block
            copies.append(remote(edge_send.at[e, i], edge_recv.at[e, i], s_edge.at[e, i], r_edge.at[e, i], to))
        for i in SEND_ORDER:
            copies[i].start()
        return copies

    def arrived(copies):
        for copy in copies:
            copy.wait_recv()
        sent.extend(copies)

    def send_edges(e, x):
        side_low, side_high = pack(x[:HALO], x[HALO:])
        t_low, t_high = pack(x[:32], x[32:64])
        b_low, b_high = pack(x[64:96], x[96:])
        return exchange(
            e, x[:HALO], x[HALO:], side_low, side_high, (t_low, t_high, b_low, b_high),
            (left, right, up_left, up_right, down_left, down_right),
        )

    def take_edges(e, x, copies):
        wide[0, HALO : HALO + K] = x
        first = jnp.where(t >= TILE_COLS, 1.0, 0.0)
        last = jnp.where(t < tiles - TILE_COLS, 1.0, 0.0)
        arrived(copies[6:])
        a, b = unpack(edge_recv[e, 2], edge_recv[e, 3])
        wide[1, HALO:K] = a
        wide[1, K : K + HALO] = b
        arrived(copies[4:6])
        wide[0, HALO + K :] = edge_recv[e, 0] * last
        wide[0, :HALO] = edge_recv[e, 1] * first
        arrived(copies[:4])
        a, b = unpack(corner_recv[e, 0], corner_recv[e, 1])
        wide[1, 192:224] = a * last
        wide[1, 224:256] = b * last
        a, b = unpack(corner_recv[e, 2], corner_recv[e, 3])
        wide[1, 0:32] = a * first
        wide[1, 32:64] = b * first

    def fold(e, inner, outer, after=()):
        side_low, side_high = pack(outer[HALO:K], outer[K : K + HALO])
        t_low, t_high = pack(outer[0:32], outer[32:64])
        b_low, b_high = pack(outer[192:224], outer[224:256])
        copies = exchange(
            e, inner[:HALO], inner[K + HALO :], side_low, side_high, (t_low, t_high, b_low, b_high),
            (right, left, up_right, up_left, down_right, down_left),
        )
        for copy in after:
            copy.start()
        arrived(copies[6:])
        a, b = unpack(edge_recv[e, 2], edge_recv[e, 3])
        arrived(copies[4:6])
        top = inner[HALO:K] + edge_recv[e, 1] + a
        bottom = inner[K : K + HALO] + edge_recv[e, 0] + b
        arrived(copies[:4])
        ta, tb = unpack(corner_recv[e, 2], corner_recv[e, 3])
        ba, bb = unpack(corner_recv[e, 0], corner_recv[e, 1])
        top = top + jnp.concatenate([ta, tb], axis=0)
        bottom = bottom + jnp.concatenate([ba, bb], axis=0)
        return jnp.concatenate([top, bottom], axis=0)

    def window(n, q):
        r = pos[0, n * 2 + q]
        c = pos[1, n * 2 + q]
        rows = both(wide[0, pl.ds(r, K), :], wide[1, pl.ds(r, K), :])
        return pltpu.roll(rows, lax.rem(EXT + HALO - c, EXT), axis=1)[:, :K]

    def send_windows(n):
        copies = [
            remote(
                win_send.at[n, 0 if j == same[n] else 1], win.at[n, plane],
                s_win.at[n, j - 1], r_win.at[n, j - 1], group[j],
            )
            for j in (1, 2, 3)
        ]
        own = window(n, pattern[n])
        if same[n] == 2:
            win_send[n, 0] = own
            copies[1].start()
        win_send[n, 1] = window(n, 1 - pattern[n])
        copies[2].start()
        copies[swap[n] - 1].start()
        if same[n] == 1:
            win_send[n, 0] = own
            copies[0].start()
        win[n, plane] = own
        return copies

    def place(n, q, g):
        r = pos[0, n * 2 + q]
        c = pos[1, n * 2 + q]
        padded = both(g, jnp.zeros((K, K), f32))
        a, b = halves(pltpu.roll(padded, lax.rem(c + EXT - HALO, EXT), axis=1))
        placed[0, K : 2 * K] = a
        placed[1, K : 2 * K] = b
        rows = pl.ds(K - r, EXT)
        return placed[0, rows, :], placed[1, rows, :]

    def tab(which):
        hi = table[which, 0:EXT]
        return jnp.concatenate([hi, hi, table[which, EXT:]], axis=0)

    pl.semaphore_wait(barrier, len(partners))
    probe_copies = [
        remote(probe.at[pl.ds(0, 4)], probe.at[pl.ds(4, 4)], s_probe.at[0], r_probe.at[0], group[1]),
    ] + [
        remote(probe.at[i], probe.at[8 + i], s_probe.at[1 + i], r_probe.at[1 + i], group[2])
        for i in range(4)
    ]
    sent = []
    pending = []
    load_plane.wait()
    first_copies = send_edges(0, plane_now[...])
    load_probe.wait()
    probe_copies[0].start()
    load_phase.wait()
    angle = phase[...].T
    prop[0] = jnp.cos(angle)
    prop[1] = jnp.sin(angle)
    for half in range(2):
        placed[half] = jnp.zeros((384, K), f32)
    load_meas.wait()
    load_pos.wait()
    load_table.wait()
    take_edges(0, plane_now[...], first_copies)
    win_copies = send_windows(0)

    for n in range(STEPS):
        meas_n = meas[n * 2 + pattern[n]].T

        def mode(j):
            at = j if n == 0 or j < 4 else j + 4
            return probe[at, 0], probe[at, 1]

        def wait_windows(n, s):
            @pl.when(core == s)
            def _():
                win_copies[1].wait_recv()

            @pl.when(core != s)
            def _():
                win_copies[0].wait_recv()
                win_copies[2].wait_recv()

            if s == 1:
                sent.extend(win_copies)

        def f1(j):
            re, im = mul((1.0 + win[n, 0], win[n, 1]), mode(j))
            work[j] = turned(times(both(re, im), tab(0)))

        def f2(j):
            y = halves(times(work[j], tab(0)))
            work[j] = both(*mul((prop[0], prop[1]), y))

        def f3(j):
            work[j] = turned(times(work[j], tab(1)))

        def f4(j):
            y = times(work[j], tab(1))
            mid[j] = y
            work[j] = both(*mul((1.0 + win[n, 2], win[n, 3]), halves(y)))

        def f5(j):
            work[j] = turned(times(work[j], tab(0)))

        def f6(j):
            y = times(work[j], tab(0))
            psi[j] = y
            re, im = halves(y)
            if j == 0:
                part[n] = re * re + im * im
            else:
                part[n] += re * re + im * im

        if n == 0:
            probe_copies[1].start()
        arrived(probe_copies[1:] if n else probe_copies[:1])
        for stage in (f1, f2, f3, f4, f5, f6):
            if stage is f1:
                wait_windows(n, 0)
            if stage is f4:
                wait_windows(n, 1)
            for j in range(WAVES):
                stage(j)

        send_part = remote(part.at[n], part_recv.at[n], s_part.at[n], r_part.at[n], group[same[n]])
        send_part.start()
        arrived([send_part])
        if n == 0:
            probe_copies[2].start()
        intensity = part[n] + part_recv[n]
        residual = intensity - meas_n
        inten[n] = intensity.T

        def b1(j):
            work[j] = turned(times(both(residual, residual) * psi[j], tab(1)))

        def b2(j):
            g = halves(times(work[j], tab(1)))
            re, im = conj_mul(halves(mid[j]), g)
            if j == 0:
                grad[n, 2] = re
                grad[n, 3] = im
            else:
                grad[n, 2] += re
                grad[n, 3] += im
            work[j] = both(*conj_mul((1.0 + win[n, 2], win[n, 3]), g))

        def b3(j):
            work[j] = turned(times(work[j], tab(0)))

        def b4(j):
            y = halves(times(work[j], tab(0)))
            work[j] = both(*conj_mul((prop[0], prop[1]), y))

        def b5(j):
            work[j] = turned(times(work[j], tab(1)))

        def b6(j):
            g = halves(times(work[j], tab(1)))
            re, im = conj_mul(mode(j), g)
            if j == 0:
                grad[n, 0] = re
                grad[n, 1] = im
            else:
                grad[n, 0] += re
                grad[n, 1] += im

        grad_copies = [
            remote(
                grad.at[n, plane_of(mate[j])], grad_recv.at[n, j - 1],
                s_grad.at[n, j - 1], r_grad.at[n, j - 1], group[j],
            )
            for j in (1, 2, 3)
        ]

        for stage in (b1, b2):
            for j in range(WAVES):
                stage(j)

        @pl.when(core == 1)
        def _():
            grad_copies[1].start()

        @pl.when(core == 0)
        def _():
            grad_copies[2].start()
            grad_copies[0].start()

        for stage in (b3, b4, b5, b6):
            for j in range(WAVES):
                stage(j)

        @pl.when(core == 0)
        def _():
            grad_copies[1].start()

        @pl.when(core == 1)
        def _():
            grad_copies[2].start()
            grad_copies[0].start()

        slot = n * 2 + pattern[n]
        keep_int = pltpu.make_async_copy(inten.at[n], int_out.at[slot], out_sem.at[n])
        send_int = remote(inten.at[n], int_out.at[slot], s_int.at[n], r_int.at[n], group[swap[n]])

        a, b = same[n] - 1, swap[n] - 1
        arrived([grad_copies[0], grad_copies[a]] if a else [grad_copies[0]])
        inner, outer = place(n, pattern[n], grad[n, plane] + grad_recv[n, a])
        arrived([grad_copies[2]] if a else grad_copies[1:])
        inner2, outer2 = place(n, 1 - pattern[n], grad_recv[n, b] + grad_recv[n, 2])
        ok = row_ok()
        inner = jnp.where(ok, inner + inner2, 0.0)
        outer = jnp.where(ok, outer + outer2, 0.0)
        keep_int.start()
        total = fold(1 + 2 * n, inner, outer, probe_copies[3 + n : 4 + n] if n == 0 else [])
        send_int.start()
        pending += [keep_int, send_int]
        plane_now[...] = plane_now[...] - total
        if n + 1 < STEPS:
            x = plane_now[...]
            edges = send_edges(2 + 2 * n, x)
            probe_copies[4].start()
            take_edges(2 + 2 * n, x, edges)
            win_copies = send_windows(n + 1)

    there = obj_out.at[0, core, comp]
    for j in (3, 2, 1):
        copy = remote(plane_now, there, s_fin.at[j - 1], r_fin.at[j - 1], group[j])
        copy.start()
        pending.append(copy)
    keep_obj = pltpu.make_async_copy(plane_now, there, out_sem.at[2])
    keep_obj.start()
    pending.append(keep_obj)
    for copy in sent:
        copy.wait_send()
    for copy in pending:
        copy.wait()


def local(object_tiles, probe, propagator_phase, measured, positions):
    anywhere = pl.BlockSpec(memory_space=pl.ANY)
    in_vmem = pl.BlockSpec(memory_space=pltpu.VMEM)
    dma = pltpu.SemaphoreType.DMA
    V = pltpu.VMEM
    scratch = [
        pltpu.SMEM((2, 4), jnp.int32),
        V((2, 2 * EXT, EXT), bf16),
        V((K, K), f32),
        V((12, 2, K, K), f32),
        V((4, K, K), f32),
        V((K, K), f32),
        V((2, EXT, K), f32),
        V((2, 2, K, K), f32),
        V((2, 4, K, K), f32),
        V((WAVES, K, EXT), f32),
        V((WAVES, K, EXT), f32),
        V((WAVES, K, EXT), f32),
        V((2, K, K), f32),
        V((2, K, K), f32),
        V((2, K, K), f32),
        V((2, K, K), f32),
        V((2, 4, K, K), f32),
        V((2, 3, K, K), f32),
        V((2, 384, K), f32),
        V((4, 4, HALO, K), f32),
        V((4, 4, HALO, K), f32),
        V((4, 4, 32, K), f32),
        V((4, 4, 32, K), f32),
        dma((6,)),
        dma((3,)),
        dma((5,)), dma((5,)),
        dma((2, 3)), dma((2, 3)),
        dma((2,)), dma((2,)),
        dma((2,)), dma((2,)),
        dma((2, 3)), dma((2, 3)),
        dma((4, 4)), dma((4, 4)),
        dma((4, 4)), dma((4, 4)),
        dma((3,)), dma((3,)),
    ]
    outs = pl.pallas_call(
        kernel,
        name="ptycho",
        out_shape=(
            V(object_tiles.shape, f32),
            V(measured.shape, f32),
        ),
        in_specs=[anywhere] * 6,
        out_specs=(in_vmem, in_vmem),
        scratch_shapes=scratch,
        compiler_params=pltpu.CompilerParams(
            collective_id=0, has_side_effects=True
        ),
    )(positions.T, object_tiles, probe, propagator_phase, measured, jnp.asarray(tables()))
    return pl.pallas_call(
        hand_over,
        name="hand_over",
        out_shape=tuple(jax.ShapeDtypeStruct(x.shape, f32) for x in outs),
        in_specs=[anywhere] * 2,
        out_specs=(anywhere, anywhere),
        scratch_shapes=[dma((2,))],
        compiler_params=pltpu.CompilerParams(vmem_limit_bytes=1024 * 1024),
    )(*outs)


def hand_over(obj, inten, obj_out, int_out, sem):
    copies = [
        pltpu.make_async_copy(obj, obj_out, sem.at[0]),
        pltpu.make_async_copy(inten, int_out, sem.at[1]),
    ]
    for copy in copies:
        copy.start()
    for copy in copies:
        copy.wait()


def solution(mesh):
    return jax.shard_map(
        local,
        mesh=mesh,
        in_specs=(
            P("tile", None, None, None, None),
            P("mode", None, None, None),
            P(),
            P("tile", None, None),
            P("tile", None),
        ),
        out_specs=(P("tile", None, None, None, None), P("tile", None, None)),
        check_vma=False,
    )
```

```python
import functools
import math

import jax
import jax.numpy as jnp
import numpy as np
from jax import lax
from jax.experimental import pallas as pl
from jax.experimental.pallas import tpu as pltpu
from jax.sharding import PartitionSpec as P

K = 128
HALO = 64
EXT = 256
STEPS = 2
TILE_COLS = 8
WAVES = 8
SEND_ORDER = (0, 3, 1, 2, 4, 5, 6, 7)

MESH = pl.DeviceIdType.MESH
f32 = jnp.float32
bf16 = jnp.bfloat16


def tables():
    index = np.arange(K)
    angle = (index[:, None] * index[None, :] % K) * (2.0 * math.pi / K)
    cos = np.cos(angle) / math.sqrt(K)
    sin = -np.sin(angle) / math.sqrt(K)
    out = []
    for sign in (1.0, -1.0):
        full = np.block([[cos, sign * sin], [-sign * sin, cos]]).astype(np.float32)
        hi = full.astype(bf16)
        lo = (full - hi.astype(np.float32)).astype(bf16)
        out.append(np.concatenate([hi, lo], axis=0))
    return np.stack(out)


def halves(x):
    return x[:, :K], x[:, K:]


def both(re, im):
    return jnp.concatenate([re, im], axis=1)


def times(x, table):
    hi = x.astype(bf16)
    lo = (x - hi.astype(f32)).astype(bf16)
    return jnp.dot(
        jnp.concatenate([hi, lo, hi], axis=1), table, preferred_element_type=f32
    )


def turned(x):
    re, im = halves(x)
    return both(re.T, im.T)


def mul(a, b):
    ar, ai = a
    br, bi = b
    return ar * br - ai * bi, ar * bi + ai * br


def conj_mul(a, b):
    ar, ai = a
    br, bi = b
    return ar * br + ai * bi, ar * bi - ai * br


def swap_lanes(x):
    return pltpu.roll(x, HALO, axis=1)


def low_lanes(rows):
    return lax.broadcasted_iota(jnp.int32, (rows, K), 1) < HALO


def pack(upper, lower):
    keep = low_lanes(upper.shape[0])
    return (
        jnp.where(keep, upper, swap_lanes(lower)),
        jnp.where(keep, swap_lanes(upper), lower),
    )


def unpack(low, high):
    keep = low_lanes(low.shape[0])
    return (
        jnp.where(keep, low, swap_lanes(high)),
        jnp.where(keep, swap_lanes(low), high),
    )


def kernel(
    pos_in,
    obj_in,
    probe_in,
    phase_in,
    meas_in,
    table_in,
    obj_out,
    int_out,
    pos,
    table,
    phase,
    probe,
    meas,
    plane_now,
    wide,
    win_send,
    win,
    psi,
    mid,
    work,
    prop,
    part,
    part_recv,
    inten,
    grad,
    grad_recv,
    placed,
    edge_send,
    edge_recv,
    corner_send,
    corner_recv,
    in_sem,
    out_sem,
    s_probe, r_probe,
    s_win, r_win,
    s_part, r_part,
    s_int, r_int,
    s_grad, r_grad,
    s_edge, r_edge,
    s_corner, r_corner,
    s_fin, r_fin,
):
    tiles = lax.axis_size("tile")
    t = lax.axis_index("tile")
    m = lax.axis_index("mode")
    core = m % 2
    chip = m // 2
    comp = (chip + t // TILE_COLS) % 2
    plane = core * 2 + comp
    pattern = [core, chip]
    same = [2, 1]
    swap = [1, 2]

    def tile_at(rows, cols):
        there = lax.rem(t + tiles + rows * TILE_COLS + cols, tiles)
        return (there, (comp + there // TILE_COLS) % 2 * 2 + core)

    up, down, left, right = tile_at(-1, 0), tile_at(1, 0), tile_at(0, -1), tile_at(0, 1)
    up_left, up_right = tile_at(-1, -1), tile_at(-1, 1)
    down_left, down_right = tile_at(1, -1), tile_at(1, 1)
    mate = [None, m + 1 - 2 * core, lax.rem(m + 2, 4), 3 - m]
    group = [None] + [(t, mate[j]) for j in (1, 2, 3)]

    def plane_of(who):
        return (who % 2) * 2 + (who // 2 + t // TILE_COLS) % 2

    def remote(src, dst, send, recv, to):
        return pltpu.make_async_remote_copy(
            src_ref=src, dst_ref=dst, send_sem=send, recv_sem=recv,
            device_id=to, device_id_type=MESH,
        )

    barrier = pltpu.get_barrier_semaphore()
    partners = [up, down, left, right, up_left, up_right, down_left, down_right] + group[1:]
    for who in partners:
        pl.semaphore_signal(barrier, inc=1, device_id=who, device_id_type=MESH)

    load_plane = pltpu.make_async_copy(obj_in.at[0, core, comp], plane_now, in_sem.at[0])
    load_probe = pltpu.make_async_copy(probe_in, probe.at[pl.ds(0, 4)], in_sem.at[1])
    load_phase = pltpu.make_async_copy(phase_in, phase, in_sem.at[2])
    load_meas = pltpu.make_async_copy(meas_in, meas, in_sem.at[3])
    load_table = pltpu.make_async_copy(table_in, table, in_sem.at[4])
    load_pos = pltpu.make_async_copy(pos_in, pos, in_sem.at[5])
    for copy in (load_plane, load_pos, load_probe, load_phase, load_meas, load_table):
        copy.start()

    def row_ok():
        row = lax.broadcasted_iota(jnp.int32, (EXT, K), 0)
        first = jnp.where(t >= TILE_COLS, 0, HALO)
        last = jnp.where(t < tiles - TILE_COLS, EXT, EXT - HALO)
        return jnp.logical_and(row >= first, row < last)

    def exchange(e, top, bottom, side_low, side_high, corners, sides):
        low_side, high_side, tl, th, bl, bh = sides
        copies = []
        for i, (block, to) in enumerate(zip(corners, (tl, th, bl, bh))):
            corner_send[e, i] = block
            copies.append(remote(corner_send.at[e, i], corner_recv.at[e, i], s_corner.at[e, i], r_corner.at[e, i], to))
        for i, (block, to) in enumerate(zip((top, bottom, side_low, side_high), (up, down, low_side, high_side))):
            edge_send[e, i] = block
            copies.append(remote(edge_send.at[e, i], edge_recv.at[e, i], s_edge.at[e, i], r_edge.at[e, i], to))
        for i in SEND_ORDER:
            copies[i].start()
        return copies

    def arrived(copies):
        for copy in copies:
            copy.wait_recv()
        sent.extend(copies)

    def send_edges(e, x):
        side_low, side_high = pack(x[:HALO], x[HALO:])
        t_low, t_high = pack(x[:32], x[32:64])
        b_low, b_high = pack(x[64:96], x[96:])
        return exchange(
            e, x[:HALO], x[HALO:], side_low, side_high, (t_low, t_high, b_low, b_high),
            (left, right, up_left, up_right, down_left, down_right),
        )

    def take_edges(e, x, copies):
        wide[0, HALO : HALO + K] = x
        first = jnp.where(t >= TILE_COLS, 1.0, 0.0)
        last = jnp.where(t < tiles - TILE_COLS, 1.0, 0.0)
        arrived(copies[6:])
        a, b = unpack(edge_recv[e, 2], edge_recv[e, 3])
        wide[1, HALO:K] = a
        wide[1, K : K + HALO] = b
        arrived(copies[4:6])
        wide[0, HALO + K :] = edge_recv[e, 0] * last
        wide[0, :HALO] = edge_recv[e, 1] * first
        arrived(copies[:4])
        a, b = unpack(corner_recv[e, 0], corner_recv[e, 1])
        wide[1, 192:224] = a * last
        wide[1, 224:256] = b * last
        a, b = unpack(corner_recv[e, 2], corner_recv[e, 3])
        wide[1, 0:32] = a * first
        wide[1, 32:64] = b * first

    def fold(e, inner, outer, after=()):
        side_low, side_high = pack(outer[HALO:K], outer[K : K + HALO])
        t_low, t_high = pack(outer[0:32], outer[32:64])
        b_low, b_high = pack(outer[192:224], outer[224:256])
        copies = exchange(
            e, inner[:HALO], inner[K + HALO :], side_low, side_high, (t_low, t_high, b_low, b_high),
            (right, left, up_right, up_left, down_right, down_left),
        )
        for copy in after:
            copy.start()
        arrived(copies[6:])
        a, b = unpack(edge_recv[e, 2], edge_recv[e, 3])
        arrived(copies[4:6])
        top = inner[HALO:K] + edge_recv[e, 1] + a
        bottom = inner[K : K + HALO] + edge_recv[e, 0] + b
        arrived(copies[:4])
        ta, tb = unpack(corner_recv[e, 2], corner_recv[e, 3])
        ba, bb = unpack(corner_recv[e, 0], corner_recv[e, 1])
        top = top + jnp.concatenate([ta, tb], axis=0)
        bottom = bottom + jnp.concatenate([ba, bb], axis=0)
        return jnp.concatenate([top, bottom], axis=0)

    def window(n, q):
        r = pos[0, n * 2 + q]
        c = pos[1, n * 2 + q]
        rows = both(wide[0, pl.ds(r, K), :], wide[1, pl.ds(r, K), :])
        return pltpu.roll(rows, lax.rem(EXT + HALO - c, EXT), axis=1)[:, :K]

    def send_windows(n):
        copies = [
            remote(
                win_send.at[n, 0 if j == same[n] else 1], win.at[n, plane],
                s_win.at[n, j - 1], r_win.at[n, j - 1], group[j],
            )
            for j in (1, 2, 3)
        ]
        own = window(n, pattern[n])
        if same[n] == 2:
            win_send[n, 0] = own
            copies[1].start()
        win_send[n, 1] = window(n, 1 - pattern[n])
        copies[2].start()
        copies[swap[n] - 1].start()
        if same[n] == 1:
            win_send[n, 0] = own
            copies[0].start()
        win[n, plane] = own
        return copies

    def place(n, q, g):
        r = pos[0, n * 2 + q]
        c = pos[1, n * 2 + q]
        padded = both(g, jnp.zeros((K, K), f32))
        a, b = halves(pltpu.roll(padded, lax.rem(c + EXT - HALO, EXT), axis=1))
        placed[0, K : 2 * K] = a
        placed[1, K : 2 * K] = b
        rows = pl.ds(K - r, EXT)
        return placed[0, rows, :], placed[1, rows, :]

    def tab(which):
        hi = table[which, 0:EXT]
        return jnp.concatenate([hi, hi, table[which, EXT:]], axis=0)

    pl.semaphore_wait(barrier, len(partners))
    probe_copies = [
        remote(probe.at[pl.ds(0, 4)], probe.at[pl.ds(4, 4)], s_probe.at[0], r_probe.at[0], group[1]),
    ] + [
        remote(probe.at[i], probe.at[8 + i], s_probe.at[1 + i], r_probe.at[1 + i], group[2])
        for i in range(4)
    ]
    sent = []
    pending = []
    load_plane.wait()
    first_copies = send_edges(0, plane_now[...])
    load_probe.wait()
    probe_copies[0].start()
    load_phase.wait()
    angle = phase[...].T
    prop[0] = jnp.cos(angle)
    prop[1] = jnp.sin(angle)
    for half in range(2):
        placed[half] = jnp.zeros((384, K), f32)
    load_meas.wait()
    load_pos.wait()
    load_table.wait()
    take_edges(0, plane_now[...], first_copies)
    win_copies = send_windows(0)

    for n in range(STEPS):
        meas_n = meas[n * 2 + pattern[n]].T

        def mode(j):
            at = j if n == 0 or j < 4 else j + 4
            return probe[at, 0], probe[at, 1]

        def wait_windows(n, s):
            @pl.when(core == s)
            def _():
                win_copies[1].wait_recv()

            @pl.when(core != s)
            def _():
                win_copies[0].wait_recv()
                win_copies[2].wait_recv()

            if s == 1:
                sent.extend(win_copies)

        def f1(j):
            re, im = mul((1.0 + win[n, 0], win[n, 1]), mode(j))
            work[j] = turned(times(both(re, im), tab(0)))

        def f2(j):
            y = halves(times(work[j], tab(0)))
            work[j] = both(*mul((prop[0], prop[1]), y))

        def f3(j):
            work[j] = turned(times(work[j], tab(1)))

        def f4(j):
            y = times(work[j], tab(1))
            mid[j] = y
            work[j] = both(*mul((1.0 + win[n, 2], win[n, 3]), halves(y)))

        def f5(j):
            work[j] = turned(times(work[j], tab(0)))

        def f6(j):
            y = times(work[j], tab(0))
            psi[j] = y
            re, im = halves(y)
            if j == 0:
                part[n] = re * re + im * im
            else:
                part[n] += re * re + im * im

        if n == 0:
            probe_copies[1].start()
        arrived(probe_copies[1:] if n else probe_copies[:1])
        for stage in (f1, f2, f3, f4, f5, f6):
            if stage is f1:
                wait_windows(n, 0)
            if stage is f4:
                wait_windows(n, 1)
            for j in range(WAVES):
                stage(j)

        send_part = remote(part.at[n], part_recv.at[n], s_part.at[n], r_part.at[n], group[same[n]])
        send_part.start()
        arrived([send_part])
        if n == 0:
            probe_copies[2].start()
        intensity = part[n] + part_recv[n]
        residual = intensity - meas_n
        inten[n] = intensity.T

        def b1(j):
            work[j] = turned(times(both(residual, residual) * psi[j], tab(1)))

        def b2(j):
            g = halves(times(work[j], tab(1)))
            re, im = conj_mul(halves(mid[j]), g)
            if j == 0:
                grad[n, 2] = re
                grad[n, 3] = im
            else:
                grad[n, 2] += re
                grad[n, 3] += im
            work[j] = both(*conj_mul((1.0 + win[n, 2], win[n, 3]), g))

        def b3(j):
            work[j] = turned(times(work[j], tab(0)))

        def b4(j):
            y = halves(times(work[j], tab(0)))
            work[j] = both(*conj_mul((prop[0], prop[1]), y))

        def b5(j):
            work[j] = turned(times(work[j], tab(1)))

        def b6(j):
            g = halves(times(work[j], tab(1)))
            re, im = conj_mul(mode(j), g)
            if j == 0:
                grad[n, 0] = re
                grad[n, 1] = im
            else:
                grad[n, 0] += re
                grad[n, 1] += im

        grad_copies = [
            remote(
                grad.at[n, plane_of(mate[j])], grad_recv.at[n, j - 1],
                s_grad.at[n, j - 1], r_grad.at[n, j - 1], group[j],
            )
            for j in (1, 2, 3)
        ]

        for stage in (b1, b2):
            for j in range(WAVES):
                stage(j)

        @pl.when(core == 1)
        def _():
            grad_copies[1].start()

        @pl.when(core == 0)
        def _():
            grad_copies[2].start()
            grad_copies[0].start()

        for stage in (b3, b4, b5, b6):
            for j in range(WAVES):
                stage(j)

        @pl.when(core == 0)
        def _():
            grad_copies[1].start()

        @pl.when(core == 1)
        def _():
            grad_copies[2].start()
            grad_copies[0].start()

        slot = n * 2 + pattern[n]
        keep_int = pltpu.make_async_copy(inten.at[n], int_out.at[slot], out_sem.at[n])
        send_int = remote(inten.at[n], int_out.at[slot], s_int.at[n], r_int.at[n], group[swap[n]])

        a, b = same[n] - 1, swap[n] - 1
        arrived([grad_copies[0], grad_copies[a]] if a else [grad_copies[0]])
        inner, outer = place(n, pattern[n], grad[n, plane] + grad_recv[n, a])
        arrived([grad_copies[2]] if a else grad_copies[1:])
        inner2, outer2 = place(n, 1 - pattern[n], grad_recv[n, b] + grad_recv[n, 2])
        ok = row_ok()
        inner = jnp.where(ok, inner + inner2, 0.0)
        outer = jnp.where(ok, outer + outer2, 0.0)
        keep_int.start()
        total = fold(1 + 2 * n, inner, outer, [probe_copies[3], send_int] if n == 0 else [send_int])
        pending += [keep_int, send_int]
        plane_now[...] = plane_now[...] - total
        if n + 1 < STEPS:
            x = plane_now[...]
            edges = send_edges(2 + 2 * n, x)
            probe_copies[4].start()
            take_edges(2 + 2 * n, x, edges)
            win_copies = send_windows(n + 1)

    there = obj_out.at[0, core, comp]
    for j in (3, 2, 1):
        copy = remote(plane_now, there, s_fin.at[j - 1], r_fin.at[j - 1], group[j])
        copy.start()
        pending.append(copy)
    keep_obj = pltpu.make_async_copy(plane_now, there, out_sem.at[2])
    keep_obj.start()
    pending.append(keep_obj)
    for copy in sent:
        copy.wait_send()
    for copy in pending:
        copy.wait()


def local(object_tiles, probe, propagator_phase, measured, positions):
    anywhere = pl.BlockSpec(memory_space=pl.ANY)
    in_vmem = pl.BlockSpec(memory_space=pltpu.VMEM)
    dma = pltpu.SemaphoreType.DMA
    V = pltpu.VMEM
    scratch = [
        pltpu.SMEM((2, 4), jnp.int32),
        V((2, 2 * EXT, EXT), bf16),
        V((K, K), f32),
        V((12, 2, K, K), f32),
        V((4, K, K), f32),
        V((K, K), f32),
        V((2, EXT, K), f32),
        V((2, 2, K, K), f32),
        V((2, 4, K, K), f32),
        V((WAVES, K, EXT), f32),
        V((WAVES, K, EXT), f32),
        V((WAVES, K, EXT), f32),
        V((2, K, K), f32),
        V((2, K, K), f32),
        V((2, K, K), f32),
        V((2, K, K), f32),
        V((2, 4, K, K), f32),
        V((2, 3, K, K), f32),
        V((2, 384, K), f32),
        V((4, 4, HALO, K), f32),
        V((4, 4, HALO, K), f32),
        V((4, 4, 32, K), f32),
        V((4, 4, 32, K), f32),
        dma((6,)),
        dma((3,)),
        dma((5,)), dma((5,)),
        dma((2, 3)), dma((2, 3)),
        dma((2,)), dma((2,)),
        dma((2,)), dma((2,)),
        dma((2, 3)), dma((2, 3)),
        dma((4, 4)), dma((4, 4)),
        dma((4, 4)), dma((4, 4)),
        dma((3,)), dma((3,)),
    ]
    outs = pl.pallas_call(
        kernel,
        name="ptycho",
        out_shape=(
            V(object_tiles.shape, f32),
            V(measured.shape, f32),
        ),
        in_specs=[anywhere] * 6,
        out_specs=(in_vmem, in_vmem),
        scratch_shapes=scratch,
        compiler_params=pltpu.CompilerParams(
            collective_id=0, has_side_effects=True
        ),
    )(positions.T, object_tiles, probe, propagator_phase, measured, jnp.asarray(tables()))
    return pl.pallas_call(
        hand_over,
        name="hand_over",
        out_shape=tuple(jax.ShapeDtypeStruct(x.shape, f32) for x in outs),
        in_specs=[anywhere] * 2,
        out_specs=(anywhere, anywhere),
        scratch_shapes=[dma((2,))],
        compiler_params=pltpu.CompilerParams(vmem_limit_bytes=1024 * 1024),
    )(*outs)


def hand_over(obj, inten, obj_out, int_out, sem):
    copies = [
        pltpu.make_async_copy(obj, obj_out, sem.at[0]),
        pltpu.make_async_copy(inten, int_out, sem.at[1]),
    ]
    for copy in copies:
        copy.start()
    for copy in copies:
        copy.wait()


def solution(mesh):
    return jax.shard_map(
        local,
        mesh=mesh,
        in_specs=(
            P("tile", None, None, None, None),
            P("mode", None, None, None),
            P(),
            P("tile", None, None),
            P("tile", None),
        ),
        out_specs=(P("tile", None, None, None, None), P("tile", None, None)),
        check_vma=False,
    )
```
